256 devices in a mesh: section: 4 (over x_lo, core), expert: 64 (over x_hi, y, z).
Axes of the slice: x: 4 (x_hi: 2, x_lo: 2; x = x_hi * 2 + x_lo), y: 4, z: 8, core: 2. Of those that a mesh axis runs over, the one named last changes fastest.
Arguments:
- x_forward: bfloat16 [4, 512, 7168], P('section', 'expert'), may hold values from -6 to 6
- route_forward: int32 [4, 512, 2], P('section', 'expert'), may hold values from 0 to 7, all different within a row; in each aligned block of 8 rows (0 to 7, 8 to 15, ..., all dimensions but the last counted through in order) at most 3 rows name the same one
- gate_forward: float32 [4, 512, 2], P('section', 'expert'), may hold values from 0.2 to 1
- x_backward: bfloat16 [4, 512, 7168], P('section', 'expert'), may hold values from -6 to 6
- grad_output: bfloat16 [4, 512, 7168], P('section', 'expert'), may hold values from -6 to 6
- route_backward: int32 [4, 512, 2], P('section', 'expert'), may hold values from 0 to 7, all different within a row; in each aligned block of 8 rows (0 to 7, 8 to 15, ..., all dimensions but the last counted through in order) at most 3 rows name the same one
- gate_backward: float32 [4, 512, 2], P('section', 'expert'), may hold values from 0.2 to 1
- w_gate: bfloat16 [4, 7168, 16384], P('section', None, 'expert'), may hold values from -0.0625 to 0.0625
- w_up: bfloat16 [4, 7168, 16384], P('section', None, 'expert'), may hold values from -0.0625 to 0.0625
- w_down: bfloat16 [4, 16384, 7168], P('section', 'expert'), may hold values from -0.125 to 0.125
Outputs:
- forward_sent: bfloat16 [4, 512, 7168], P('section', 'expert')
- backward_sent: bfloat16 [4, 512, 7168], P('section', 'expert')
The draws below stay inside these ranges and needn't reach their ends.
Inputs may be any that keep to these rules, and one draw needn't show every extreme that they name: `route_forward`: in each aligned block of 8 tokens a token names 2 different experts, no expert is named by more than 3 tokens of the block, a bound that some block reaches. `route_backward`: as for route_forward.
All inputs are finite; a program needn't handle non-finite values.
Results may differ from the reference program's by a relative error of at most 0.007.
Values may be sent and summed in bfloat16 or wider, within the bound.
A program may use at most 128 MiB of HBM per device.

```python
import math
import jax
import jax.numpy as jnp
import numpy as np
from jax import lax

D = 7168
HID = 2048
GROUP = 8
HID_DEV = 256
T_DEV = 8
EXPERTS = 8
TOP = 2
CAP = 3
TOKENS = 512
HID_ALL = 16384
N_SECTION = 4
N_EXPERT = 64


def block_scale(own_key, extent, split, low, largest):
    gain, own = 1.0, jax.random.fold_in(own_key, 6)
    for dim, parts in split:
        steps = jnp.exp(jax.random.uniform(jax.random.fold_in(own, dim), (parts,), jnp.float32, low / len(split), largest / len(split)))
        gain = gain * jnp.repeat(steps, extent[dim] // parts).reshape([-1 if axis == dim else 1 for axis in range(len(extent))])
    return gain


def routed_block(stream_key, own, number, rows, count, top, most, lean):
    order = jax.random.permutation(stream_key, count)
    heavy_load, common = portions_of(count, rows * top, most, lean, True), portions_of(count, rows * top, most, lean, False)
    places = jnp.arange(count)

    def named(tallies, turn):
        used = int((tallies > 0).sum())
        fixed = max(1, used // 4)
        moved = fixed + (places - fixed + turn * (used - fixed)) % max(1, count - fixed)
        return jnp.zeros((count,), jnp.int32).at[order[jnp.where(places < fixed, places, moved)]].set(jnp.asarray(tallies, jnp.int32))

    tallies = jnp.where(number % 4 == 0, named(heavy_load, number // 4), named(common, number - number // 4 - 1))
    mixed = jax.random.permutation(jax.random.fold_in(own, 3), count)
    donor, sink = mixed[0:count // 2 * 2:2], mixed[1:count // 2 * 2:2]
    slack = jnp.minimum(tallies[donor] - 1, most - tallies[sink]) // 2
    slack = jnp.where((donor == order[0]) | (sink == order[0]) | (tallies[sink] == 0), 0, jnp.maximum(slack, 0))
    moved = jax.random.randint(jax.random.fold_in(own, 4), (count // 2,), 0, 1 << 20) % (slack + 1)
    tallies = tallies.at[donor].add(-moved).at[sink].add(moved)
    members = jnp.searchsorted(jnp.cumsum(tallies), jnp.arange(rows * top), side="right").astype(jnp.int32)
    listing = members.reshape(top, rows).T
    listing = listing[jax.random.permutation(jax.random.fold_in(own, 1), rows)]
    turn = jax.random.randint(jax.random.fold_in(own, 2), (rows, 1), 0, top)
    return jnp.take_along_axis(listing, (jnp.arange(top)[None, :] + turn) % top, axis=1)


def portions_of(number_of, total, bound, slope, full):
    portions = [(1 << 20) // math.isqrt(standing ** slope) + 1 for standing in range(1, number_of + 1)]
    largest = bound if full else min(bound, max(-(-total // number_of), total * portions[0] // sum(portions)))
    least = 1 if total - largest >= number_of - 1 else 0
    counts, spare = [largest] + [least] * (number_of - 1), total - largest - least * (number_of - 1)
    while spare > 0:
        movable = [i for i in range(1, number_of) if counts[i] < largest] or [i for i in range(1, number_of) if counts[i] < bound]
        mass, remaining = sum([portions[i] for i in movable]), spare
        for i in movable:
            addition = min(bound - counts[i], max(1, remaining * portions[i] // mass), spare)
            counts[i] = counts[i] + addition
            spare = spare - addition
    return np.array(counts)


def bell_draw(key, shape, scale, bound, shards=(), kind=jnp.bfloat16):
    array = scale * jax.random.normal(key, shape, jnp.float32)
    if shards:
        array = array * block_scale(key, shape, shards, -0.22, 0.18)
    return jnp.clip(array, -bound, bound).astype(kind)


def setup_inputs(seed: int = 0) -> dict:
    arg_keys = jax.random.split(jax.random.key(seed), 11)
    x_forward = bell_draw(arg_keys[0], (N_SECTION, TOKENS, D), 1.0, 6.0, ((0, 4), (1, 64)))
    route_forward_keys = jax.random.split(jax.random.fold_in(arg_keys[1], 1), N_SECTION * TOKENS // T_DEV)
    route_forward_turns = jax.random.permutation(jax.random.fold_in(arg_keys[1], 3), N_SECTION * TOKENS // T_DEV)
    route_forward = jax.vmap(lambda own, number: routed_block(jax.random.fold_in(arg_keys[1], 2), own, number, T_DEV, EXPERTS, TOP, CAP, 2))(route_forward_keys, route_forward_turns).reshape((N_SECTION, TOKENS, TOP))
    gate_forward = jnp.clip(0.2 + 0.8 * jax.random.uniform(arg_keys[2], (N_SECTION, TOKENS, TOP), jnp.float32) ** block_scale(arg_keys[2], (N_SECTION, TOKENS, TOP), ((0, 4), (1, 64)), -0.2, 0.2), 0.2, 1.0)
    x_backward = bell_draw(arg_keys[3], (N_SECTION, TOKENS, D), 1.0, 6.0, ((0, 4), (1, 64)))
    grad_output = bell_draw(arg_keys[4], (N_SECTION, TOKENS, D), 1.0, 6.0, ((0, 4), (1, 64)))
    route_backward_keys = jax.random.split(jax.random.fold_in(arg_keys[5], 1), N_SECTION * TOKENS // T_DEV)
    route_backward_turns = jax.random.permutation(jax.random.fold_in(arg_keys[5], 3), N_SECTION * TOKENS // T_DEV)
    route_backward = jax.vmap(lambda own, number: routed_block(jax.random.fold_in(arg_keys[5], 2), own, number, T_DEV, EXPERTS, TOP, CAP, 2))(route_backward_keys, route_backward_turns).reshape((N_SECTION, TOKENS, TOP))
    gate_backward = jnp.clip(0.2 + 0.8 * jax.random.uniform(arg_keys[6], (N_SECTION, TOKENS, TOP), jnp.float32) ** block_scale(arg_keys[6], (N_SECTION, TOKENS, TOP), ((0, 4), (1, 64)), -0.2, 0.2), 0.2, 1.0)
    w_gate = bell_draw(arg_keys[7], (N_SECTION, D, HID_ALL), D ** -0.5, 0.0625, ((0, 4), (2, 64)))
    w_up = bell_draw(arg_keys[8], (N_SECTION, D, HID_ALL), D ** -0.5, 0.0625, ((0, 4), (2, 64)))
    w_down = bell_draw(arg_keys[9], (N_SECTION, HID_ALL, D), HID ** -0.5, 0.125, ((0, 4), (1, 64)))
    return dict(x_forward=x_forward, route_forward=route_forward, gate_forward=gate_forward, x_backward=x_backward, grad_output=grad_output, route_backward=route_backward, gate_backward=gate_backward, w_gate=w_gate, w_up=w_up, w_down=w_down)


def tables(route, gates, experts, cap):
    top = route.shape[-1]
    flat = route.reshape(-1)
    count = flat.shape[0]
    expert_hot = (flat[:, None] == jnp.arange(experts, dtype=jnp.int32)[None, :]).astype(jnp.int32)
    ranks = jnp.cumsum(expert_hot, axis=0) - 1
    slot = jnp.sum(ranks * expert_hot, axis=1)
    position = flat * cap + slot
    place_hot = (position[:, None] == jnp.arange(experts * cap, dtype=jnp.int32)[None, :]).astype(jnp.float32)
    owner = jnp.arange(count, dtype=jnp.int32) // top
    token_hot = (owner[:, None] == jnp.arange(count // top, dtype=jnp.int32)[None, :]).astype(jnp.float32)
    select = jnp.dot(place_hot.T, token_hot, precision=lax.Precision.HIGHEST)
    weights = jnp.dot(token_hot.T, place_hot * gates.reshape(-1)[:, None], precision=lax.Precision.HIGHEST)
    return select, weights


def gather_rows(select, rows):
    buffer = jnp.einsum("sqt,std->sqd", select, rows.astype(jnp.float32), precision=lax.Precision.HIGHEST)
    buffer = buffer.astype(jnp.bfloat16).reshape(N_EXPERT, EXPERTS, CAP, D)
    return jnp.transpose(buffer, (1, 0, 2, 3)).reshape(EXPERTS, N_EXPERT * CAP, D)


def spread(weights, result, base):
    result = jnp.transpose(result.reshape(EXPERTS, N_EXPERT, CAP, D), (1, 0, 2, 3)).reshape(N_EXPERT, EXPERTS * CAP, D)
    total = base.astype(jnp.float32) + jnp.einsum("stq,sqd->std", weights, result, precision=lax.Precision.HIGHEST)
    return total.astype(jnp.bfloat16)


def one_section(inputs):
    (x_f, r_f, g_f, x_b, d_y, r_b, g_b, w_g, w_u, w_d) = inputs
    sel_f, wts_f = jax.vmap(lambda r, g: tables(r, g, EXPERTS, CAP))(r_f.reshape(N_EXPERT, T_DEV, TOP), g_f.reshape(N_EXPERT, T_DEV, TOP))
    sel_b, wts_b = jax.vmap(lambda r, g: tables(r, g, EXPERTS, CAP))(r_b.reshape(N_EXPERT, T_DEV, TOP), g_b.reshape(N_EXPERT, T_DEV, TOP))
    xs_f = x_f.reshape(N_EXPERT, T_DEV, D)
    xs_b = x_b.reshape(N_EXPERT, T_DEV, D)
    dys = d_y.reshape(N_EXPERT, T_DEV, D)
    rows_f = gather_rows(sel_f, xs_f)
    rows_b = gather_rows(sel_b, xs_b)
    rows_d = gather_rows(sel_b, dys)
    gate_cols = jnp.transpose(w_g.reshape(D, EXPERTS, HID), (1, 0, 2))
    up_cols = jnp.transpose(w_u.reshape(D, EXPERTS, HID), (1, 0, 2))
    down_rows = w_d.reshape(EXPERTS, HID, D)

    def expert(items):
        (rf, rb, rd, wg, wu, wd) = items
        count = rf.shape[0]
        a = jnp.dot(rf, wg, preferred_element_type=jnp.float32)
        b = jnp.dot(rf, wu, preferred_element_type=jnp.float32)
        hidden = (jax.nn.silu(a) * b).astype(jnp.bfloat16)
        part = jnp.einsum("rgh,ghd->rgd", hidden.reshape(count, GROUP, HID_DEV).astype(jnp.float32), wd.reshape(GROUP, HID_DEV, D).astype(jnp.float32))
        out_f = jnp.sum(part.astype(jnp.bfloat16).astype(jnp.float32), axis=1)
        a2 = jnp.dot(rb, wg, preferred_element_type=jnp.float32)
        b2 = jnp.dot(rb, wu, preferred_element_type=jnp.float32)
        dh = jnp.dot(rd, wd.T, preferred_element_type=jnp.float32)
        sig = jax.nn.sigmoid(a2)
        d_a = (dh * b2 * sig * (1.0 + a2 * (1.0 - sig))).astype(jnp.bfloat16)
        d_b = (dh * a2 * sig).astype(jnp.bfloat16)
        back = jnp.einsum("rgh,dgh->rgd", d_a.reshape(count, GROUP, HID_DEV).astype(jnp.float32), wg.reshape(D, GROUP, HID_DEV).astype(jnp.float32))
        back = back + jnp.einsum("rgh,dgh->rgd", d_b.reshape(count, GROUP, HID_DEV).astype(jnp.float32), wu.reshape(D, GROUP, HID_DEV).astype(jnp.float32))
        out_b = jnp.sum(back.astype(jnp.bfloat16).astype(jnp.float32), axis=1)
        return out_f, out_b

    res_f, res_b = lax.map(expert, (rows_f, rows_b, rows_d, gate_cols, up_cols, down_rows))
    out = spread(wts_f, res_f, xs_f).reshape(TOKENS, D)
    grad = spread(wts_b, res_b, dys).reshape(TOKENS, D)
    return out, grad


def reference(x_forward, route_forward, gate_forward, x_backward, grad_output, route_backward, gate_backward, w_gate, w_up, w_down):
    outs, grads = lax.map(one_section, (x_forward, route_forward, gate_forward, x_backward, grad_output, route_backward, gate_backward, w_gate, w_up, w_down))
    return jnp.roll(outs, 1, axis=0), jnp.roll(grads, -1, axis=0)
```

```python
import jax
import jax.numpy as jnp
from jax import lax
from jax.sharding import PartitionSpec as P

GROUP = 8


def passed_along(block, axis, distance):
    devices = range(lax.axis_size(axis))
    route = [((i - distance) % len(devices), i) for i in devices]
    return lax.ppermute(block, axis, route)


def tables(route, gates, experts, cap):
    top = route.shape[-1]
    flat = route.reshape(-1)
    count = flat.shape[0]
    expert_hot = (flat[:, None] == jnp.arange(experts, dtype=jnp.int32)[None, :]).astype(jnp.int32)
    ranks = jnp.cumsum(expert_hot, axis=0) - 1
    slot = jnp.sum(ranks * expert_hot, axis=1)
    position = flat * cap + slot
    place_hot = (position[:, None] == jnp.arange(experts * cap, dtype=jnp.int32)[None, :]).astype(
        jnp.float32
    )
    owner = jnp.arange(count, dtype=jnp.int32) // top
    token_hot = (owner[:, None] == jnp.arange(count // top, dtype=jnp.int32)[None, :]).astype(
        jnp.float32
    )
    select = jnp.dot(place_hot.T, token_hot, precision=lax.Precision.HIGHEST)
    weights = jnp.dot(
        token_hot.T, place_hot * gates.reshape(-1)[:, None], precision=lax.Precision.HIGHEST
    )
    return (select, weights)


def on_device(
    x_forward,
    route_forward,
    gate_forward,
    x_backward,
    grad_output,
    route_backward,
    gate_backward,
    w_gate,
    w_up,
    w_down,
):
    devices = lax.axis_size("expert")
    experts = devices // GROUP
    tok_here = x_forward.shape[1]
    width = x_forward.shape[2]
    top = route_forward.shape[2]
    cap = min(tok_here, 3 * tok_here * top // (2 * experts))
    wg = w_gate[0]
    wu = w_up[0]
    wd = w_down[0]
    sel_f, wts_f = tables(route_forward[0], gate_forward[0], experts, cap)
    sel_b, wts_b = tables(route_backward[0], gate_backward[0], experts, cap)

    plane = [[e * GROUP + m for e in range(experts)] for m in range(GROUP)]
    line = [[e * GROUP + m for m in range(GROUP)] for e in range(experts)]

    def pack(select, rows):
        send = jnp.dot(
            select.astype(jnp.bfloat16), rows, preferred_element_type=jnp.float32
        ).astype(jnp.bfloat16)
        return send.reshape(experts, cap, width)

    def deliver(send):
        here = lax.all_to_all(
            send, "expert", split_axis=0, concat_axis=0, axis_index_groups=plane, tiled=True
        )
        flat = here.reshape(experts * cap, -1)
        return lax.all_gather(flat, "expert", axis=0, axis_index_groups=line, tiled=True)

    def give_back(part):
        summed = lax.psum_scatter(
            part, "expert", scatter_dimension=0, axis_index_groups=line, tiled=True
        )
        return lax.all_to_all(
            summed.reshape(experts, cap, width),
            "expert",
            split_axis=0,
            concat_axis=0,
            axis_index_groups=plane,
            tiled=True,
        )

    def spread(weights, result, base):
        total = result.astype(jnp.float32).reshape(experts * cap, width)
        summed = jnp.dot(weights, total, precision=lax.Precision.HIGHEST)
        return (base.astype(jnp.float32) + summed).astype(jnp.bfloat16)

    rows = deliver(pack(sel_f, x_forward[0]))
    a_pre = jnp.dot(rows, wg, preferred_element_type=jnp.float32)
    b_pre = jnp.dot(rows, wu, preferred_element_type=jnp.float32)
    hidden = (jax.nn.silu(a_pre) * b_pre).astype(jnp.bfloat16)
    part = jnp.dot(hidden, wd, preferred_element_type=jnp.float32).astype(jnp.bfloat16)
    result_f = give_back(part)
    both = jnp.concatenate([pack(sel_b, x_backward[0]), pack(sel_b, grad_output[0])], axis=2)
    both = deliver(both)
    rows = both[:, :width]
    grads = both[:, width:]
    a_pre = jnp.dot(rows, wg, preferred_element_type=jnp.float32)
    b_pre = jnp.dot(rows, wu, preferred_element_type=jnp.float32)
    d_hidden = lax.dot_general(
        grads, wd, (((1,), (1,)), ((), ())), preferred_element_type=jnp.float32
    )
    sig = jax.nn.sigmoid(a_pre)
    d_a = (d_hidden * b_pre * sig * (1.0 + a_pre * (1.0 - sig))).astype(jnp.bfloat16)
    d_b = (d_hidden * a_pre * sig).astype(jnp.bfloat16)
    back = lax.dot_general(d_a, wg, (((1,), (1,)), ((), ())), preferred_element_type=jnp.float32)
    back = back + lax.dot_general(
        d_b, wu, (((1,), (1,)), ((), ())), preferred_element_type=jnp.float32
    )
    result_b = give_back(back.astype(jnp.bfloat16))
    out = spread(wts_f, result_f, x_forward[0])
    grad = spread(wts_b, result_b, grad_output[0])
    forward_sent = passed_along(out[None], "section", 1)
    backward_sent = passed_along(grad[None], "section", -1)
    return (forward_sent, backward_sent)


def solution(mesh):
    in_specs = (
        P("section", "expert", None),
        P("section", "expert", None),
        P("section", "expert", None),
        P("section", "expert", None),
        P("section", "expert", None),
        P("section", "expert", None),
        P("section", "expert", None),
        P("section", None, "expert"),
        P("section", None, "expert"),
        P("section", "expert", None),
    )
    out_specs = (P("section", "expert", None), P("section", "expert", None))
    return jax.shard_map(
        on_device, mesh=mesh, in_specs=in_specs, out_specs=out_specs, check_vma=False
    )
```
